32 devices in a mesh: section: 2 (over x), dp: 16 (over z, y, core).
Axes of the slice: x: 2, y: 2, z: 4, core: 2. Of those that a mesh axis runs over, the one named last changes fastest.
Arguments:
- tokens_in: bfloat16 [3, 1024, 1024], P(None, 'dp'), may hold values from -6 to 6
- out_cotangent: bfloat16 [3, 1024, 1024], P(None, 'dp'), may hold values from -6 to 6
- in_weight: bfloat16 [2, 1024, 4384], P('section', 'dp'), may hold values from -0.1875 to 0.1875
- out_weight: bfloat16 [2, 2048, 1024], P('section', 'dp'), may hold values from -0.125 to 0.125
- norm_gain: float32 [2, 1024], P('section'), may hold values from 0.5 to 1.5
- conv_weight: float32 [2, 4, 2304], P('section'), may hold values from -3 to 3
- conv_bias: float32 [2, 2304], P('section'), may hold values from -3 to 3
- dt_bias: float32 [2, 32], P('section'), may hold values from -4 to 0
- a_log: float32 [2, 32], P('section'), may hold values from 0 to 2.77
- skip_gain: float32 [2, 32], P('section'), may hold values from 0.5 to 1.5
- gate_gain: float32 [2, 2048], P('section'), may hold values from 0.5 to 1.5
- group_fill: int32 [3, 32], P(None, 'dp'), may hold values from 0 to 32, as said below
- group_link: int32 [3, 32], P(None, 'dp'), may hold values from 0 to 1, as said below
Outputs:
- section_outputs: float32 [2, 3, 1024, 1024], P('section', None, 'dp')
- section_input_grads: float32 [2, 3, 1024, 1024], P('section', None, 'dp')
- grad_in_weight: float32 [2, 1024, 4384], P('section', 'dp')
- grad_out_weight: float32 [2, 2048, 1024], P('section', 'dp')
- grad_norm_gain: float32 [2, 1024], P('section')
- grad_conv_weight: float32 [2, 4, 2304], P('section')
- grad_conv_bias: float32 [2, 2304], P('section')
- grad_dt_bias: float32 [2, 32], P('section')
- grad_a_log: float32 [2, 32], P('section')
- grad_skip_gain: float32 [2, 32], P('section')
- grad_gate_gain: float32 [2, 2048], P('section')
The draws below stay inside these ranges and needn't reach their ends.
Inputs may be any that keep to these rules, and one draw needn't show every extreme that they name: `group_fill`: each slot's groups hold whole sequences from the start of a group: a sequence fills groups, the last one from its start to its end, the rest of that group is unused; some groups are empty, and how many differs from slot to slot. Some group of every micro-batch is full. `group_link`: A link of 1 stands only on a group that is not the first of its slot, follows a full group and holds a token; every micro-batch has one.
All inputs are finite; a program needn't handle non-finite values.
Results may differ from the reference program's by a relative error of at most 0.0097.
Values may be sent and summed in bfloat16 or wider, within the bound.
No kernel may reach another device: no remote copies, remote signals or barrier semaphores. Data moves between devices by JAX's collectives and lax.ppermute only.
A program may use at most 128 MiB of HBM per device.

```python
import jax
import jax.numpy as jnp
from jax import lax

D = 1024
INNER = 2048
HEADS = 32
KCONV = 4
GROUP = 32
NC = 2
MICRO = 3
CONV = 2304
ZX = 4384
TOKENS = 1024
GROUPS_ALL = 32
N_SECTION = 2
N_DP = 16


def slot_layout(key):
    base_key = jax.random.fold_in(key, 11)
    key_kind, key_part, key_level, key_vacant, key_coin = jax.random.split(base_key, 5)
    slot_count = GROUPS_ALL // NC
    arrangement_shape = (MICRO, slot_count, NC)
    kinds = jax.random.randint(key_kind, arrangement_shape, 0, 3)
    partial_fill = jax.random.randint(key_part, arrangement_shape, 1, GROUP)
    padding_values = jnp.where(kinds == 0, partial_fill, GROUP)
    level_values = jax.random.randint(key_level, (MICRO, slot_count, 1), 0, 3)
    empty_slots = jax.random.randint(key_vacant, arrangement_shape, 0, 3) < level_values
    padding_values = jnp.where(empty_slots, 0, padding_values)
    padding_values = padding_values.at[:, 0, 0].set(GROUP)
    padding_values = padding_values.at[:, 0, 1].set(jnp.maximum(padding_values[:, 0, 1], 1))
    previous_full = jnp.concatenate([jnp.zeros((MICRO, slot_count, 1), jnp.int32), (padding_values[:, :, :-1] == GROUP).astype(jnp.int32)], axis=2)
    coins = jax.random.randint(key_coin, arrangement_shape, 0, 2)
    link_values = previous_full * (padding_values > 0).astype(jnp.int32) * coins
    link_values = link_values.at[:, 0, 1].set(1)
    return (padding_values.reshape(MICRO, GROUPS_ALL).astype(jnp.int32), link_values.reshape(MICRO, GROUPS_ALL).astype(jnp.int32))


def draw_group_fill(key, part):
    return slot_layout(key)[0]


def draw_group_link(key, part):
    return slot_layout(key)[1]


def with_spikes(drawn, own_key, source, target, blocks, factor):
    owner, partner = [(jnp.arange(drawn.shape[axis_at]) // (drawn.shape[axis_at] // blocks)).reshape([-1 if axis == axis_at else 1 for axis in range(drawn.ndim)]) for axis_at in (source, target)]
    chosen = jax.random.permutation(own_key, blocks)[partner]
    strong = (owner == chosen) | (owner == (partner + blocks // 2) % blocks)
    return jnp.where(strong, factor * drawn, drawn)


def block_levels(key, shape, pieces, low, largest):
    def one(axis_at, shards_of):
        draws = jax.random.uniform(jax.random.fold_in(jax.random.fold_in(key, 6), axis_at), (shards_of,), jnp.float32, low / len(pieces), largest / len(pieces))
        return jnp.repeat(jnp.exp(draws), shape[axis_at] // shards_of).reshape((-1,) + (1,) * (len(shape) - axis_at - 1))

    level = one(*pieces[0])
    for cut in pieces[1:]:
        level = level * one(*cut)
    return level


def scatter_about(rng, shape, spread, bound, shards=(), held_as=jnp.bfloat16):
    array = spread * jax.random.normal(rng, shape, jnp.float32)
    if shards:
        array = array * block_levels(rng, shape, shards, -0.22, 0.18)
    return jnp.clip(array, -bound, bound).astype(held_as)


def heavy_noise(rng, extent, width, bound, shards, heavy, kind=jnp.bfloat16):
    values = width * jax.random.normal(rng, extent, jnp.float32)
    if shards:
        values = values * block_levels(rng, extent, shards, -0.22, 0.18)
    return jnp.clip(with_spikes(values, jax.random.fold_in(rng, 3), *heavy), -bound, bound).astype(kind)


def setup_inputs(seed: int = 0) -> dict:
    streams_of = jax.random.split(jax.random.key(seed), 14)
    return {
        "tokens_in": heavy_noise(streams_of[0], (MICRO, TOKENS, D), 1.0, 6.0, ((1, 16),), (1, 2, 16, 2.0)),
        "out_cotangent": scatter_about(streams_of[1], (MICRO, TOKENS, D), 1.0, 6.0, ((1, 16),)),
        "in_weight": scatter_about(streams_of[2], (N_SECTION, D, ZX), D ** -0.5, 0.1875, ((0, 2), (1, 16))),
        "out_weight": scatter_about(streams_of[3], (N_SECTION, INNER, D), INNER ** -0.5, 0.125, ((0, 2), (1, 16))),
        "norm_gain": jnp.clip(1.0 + 0.1 * jax.random.normal(streams_of[4], (N_SECTION, D), jnp.float32), 0.5, 1.5),
        "conv_weight": scatter_about(streams_of[5], (N_SECTION, KCONV, CONV), KCONV ** -0.5, 3.0, ((0, 2),), jnp.float32),
        "conv_bias": scatter_about(streams_of[6], (N_SECTION, CONV), 0.5, 3.0, ((0, 2),), jnp.float32),
        "dt_bias": jnp.clip(-4.0 + 4.0 * jax.random.uniform(streams_of[7], (N_SECTION, HEADS), jnp.float32) ** block_levels(streams_of[7], (N_SECTION, HEADS), ((0, 2),), -0.2, 0.2), -4.0, 0.0),
        "a_log": jnp.clip(2.77 * jax.random.uniform(streams_of[8], (N_SECTION, HEADS), jnp.float32) ** block_levels(streams_of[8], (N_SECTION, HEADS), ((0, 2),), -0.2, 0.2), 0.0, 2.77),
        "skip_gain": jnp.clip(0.5 + 1.0 * jax.random.uniform(streams_of[9], (N_SECTION, HEADS), jnp.float32) ** block_levels(streams_of[9], (N_SECTION, HEADS), ((0, 2),), -0.2, 0.2), 0.5, 1.5),
        "gate_gain": jnp.clip(1.0 + 0.1 * jax.random.normal(streams_of[10], (N_SECTION, INNER), jnp.float32), 0.5, 1.5),
        "group_fill": draw_group_fill(jax.random.fold_in(streams_of[13], 71), 0),
        "group_link": draw_group_link(jax.random.fold_in(streams_of[13], 71), 0),
    }


EPSILON = 1e-05
HIGHEST = lax.Precision.HIGHEST

def norm_map(values, gain_row):
    return values * lax.rsqrt(lax.optimization_barrier(jnp.mean(values * values, axis=-1, keepdims=True)) + EPSILON) * gain_row

def ssd_scan(x_heads, step_size, log_decay, input_b, input_c, link_row, groups):
    rows_all, head_count, head_size = x_heads.shape
    length = rows_all // groups
    state_size = input_b.shape[1]
    x_blocks = x_heads.reshape(groups, length, head_count, head_size)
    dt_blocks = step_size.reshape(groups, length, head_count)
    cumulative = jnp.cumsum(log_decay.reshape(groups, length, head_count), axis=1)
    b_blocks = input_b.reshape(groups, length, state_size)
    c_blocks = input_c.reshape(groups, length, state_size)
    scores = jnp.einsum('cin,cjn->cij', c_blocks, b_blocks, precision=HIGHEST)
    causal = jnp.arange(length)[:, None] >= jnp.arange(length)[None, :]
    decay_gap = cumulative[:, :, None, :] - cumulative[:, None, :, :]
    factors = jnp.exp(jnp.where(causal[None, :, :, None], decay_gap, -jnp.inf))
    factors = factors * scores[..., None] * dt_blocks[:, None, :, :]
    diag_out = jnp.einsum('cijh,cjhp->cihp', factors, x_blocks, precision=HIGHEST)
    group_end = cumulative[:, -1:, :]
    to_end = jnp.exp(group_end - cumulative) * dt_blocks
    group_states = jnp.einsum('cjh,cjhp,cjn->chpn', to_end, x_blocks, b_blocks, precision=HIGHEST)
    group_decay = jnp.exp(group_end[:, 0, :])
    link_float = link_row.astype(jnp.float32)
    carried = jnp.zeros((head_count, head_size, state_size), jnp.float32)
    entering = [carried]
    for group_index in range(1, groups):
        carried = link_float[group_index] * (group_decay[group_index - 1][:, None, None] * carried + group_states[group_index - 1])
        entering.append(carried)
    entering = jnp.stack(entering)
    off_out = jnp.einsum('cih,cin,chpn->cihp', jnp.exp(cumulative), c_blocks, entering, precision=HIGHEST)
    return (diag_out + off_out).reshape(rows_all, head_count, head_size)

def mixer_slot(projected, conv_weight, conv_bias, dt_bias, a_log, skip_gain, gate_gain, fill_row, link_row):
    rows_all = projected.shape[0]
    groups = fill_row.shape[0]
    length = rows_all // groups
    inner_size = gate_gain.shape[0]
    head_count = dt_bias.shape[0]
    conv_size = conv_bias.shape[0]
    state_size = (conv_size - inner_size) // 2
    head_size = inner_size // head_count
    gate_part = projected[:, :inner_size]
    conv_in = projected[:, inner_size:inner_size + conv_size]
    dt_raw = projected[:, inner_size + conv_size:]
    within = jnp.arange(rows_all) % length
    linked = jnp.broadcast_to(link_row.astype(jnp.float32)[:, None], (groups, length)).reshape(rows_all)
    filled = jnp.broadcast_to(fill_row[:, None], (groups, length)).reshape(rows_all)
    valid = (within < filled).astype(jnp.float32)
    conv_sum = conv_bias + conv_weight[0] * conv_in
    for lag_steps in range(1, conv_weight.shape[0]):
        shifted = jnp.concatenate([jnp.zeros((lag_steps, conv_size), jnp.float32), conv_in[:-lag_steps]], axis=0)
        keep_mask = jnp.maximum((within >= lag_steps).astype(jnp.float32), linked)
        conv_sum = conv_sum + conv_weight[lag_steps] * shifted * keep_mask[:, None]
    activated = jax.nn.silu(conv_sum)
    x_heads = activated[:, :inner_size].reshape(rows_all, head_count, head_size)
    input_b = activated[:, inner_size:inner_size + state_size]
    input_c = activated[:, inner_size + state_size:]
    step_size = jax.nn.softplus(dt_raw + dt_bias)
    log_decay = step_size * -jnp.exp(a_log)
    scanned = ssd_scan(x_heads, step_size, log_decay, input_b, input_c, link_row, groups)
    scanned = scanned + skip_gain[:, None] * x_heads
    gated = scanned.reshape(rows_all, inner_size) * jax.nn.silu(gate_part)
    return norm_map(gated, gate_gain) * valid[:, None]

def mixer_row_set(projected, params, fill_rows, link_rows):
    slot_count = fill_rows.shape[0]
    blocks = projected.reshape(slot_count, -1, projected.shape[1])

    def one_slot(slot_items):
        return mixer_slot(slot_items[0], *params, slot_items[1], slot_items[2])
    mixed_blocks = lax.map(one_slot, (blocks, fill_rows, link_rows))
    return mixed_blocks.reshape(projected.shape[0], -1)

def mixer_grads(projected, params, fill_rows, link_rows, d_mixed):
    slot_count = fill_rows.shape[0]
    blocks = projected.reshape(slot_count, -1, projected.shape[1])
    d_blocks = d_mixed.reshape(slot_count, -1, d_mixed.shape[1])

    def one_slot(slot_items):
        proj_block, fill_row, link_row, d_block = slot_items

        def local_map(proj_rows, *param_list):
            return mixer_slot(proj_rows, *param_list, fill_row, link_row)
        unused, pull_back = jax.vjp(local_map, proj_block, *params)
        return pull_back(d_block)
    result_list = lax.map(one_slot, (blocks, fill_rows, link_rows, d_blocks))
    d_projected = result_list[0].reshape(projected.shape)
    param_grads = tuple((lax.optimization_barrier(jnp.sum(stacked, axis=0)) for stacked in result_list[1:]))
    return (d_projected, param_grads)

def reference(tokens_in, out_cotangent, in_weight, out_weight, norm_gain, conv_weight, conv_bias, dt_bias, a_log, skip_gain, gate_gain, group_fill, group_link):
    contract_rows = (((0,), (0,)), ((), ()))
    contract_cols = (((1,), (1,)), ((), ()))
    outputs_all = [[] for section_index in range(N_SECTION)]
    input_grads = [[] for section_index in range(N_SECTION)]
    grad_in = [jnp.zeros((D, ZX), jnp.float32) for section_index in range(N_SECTION)]
    grad_out = [jnp.zeros((INNER, D), jnp.float32) for section_index in range(N_SECTION)]
    grad_gain = [jnp.zeros((D,), jnp.float32) for section_index in range(N_SECTION)]
    grad_small = [None for section_index in range(N_SECTION)]
    for batch_index in range(MICRO):
        fill_rows = group_fill[batch_index].reshape(N_DP, NC)
        link_rows = group_link[batch_index].reshape(N_DP, NC)
        layer_in = tokens_in[batch_index]
        saved = []
        for section_index in range(N_SECTION):
            params = (conv_weight[section_index], conv_bias[section_index], dt_bias[section_index], a_log[section_index], skip_gain[section_index], gate_gain[section_index])
            residual = layer_in.astype(jnp.float32)
            normed = norm_map(residual, norm_gain[section_index]).astype(jnp.bfloat16)
            projected = jnp.dot(normed, in_weight[section_index], preferred_element_type=jnp.float32)
            mixed = mixer_row_set(projected, params, fill_rows, link_rows).astype(jnp.bfloat16)
            output = residual + jnp.dot(mixed, out_weight[section_index], preferred_element_type=jnp.float32)
            outputs_all[section_index].append(output)
            saved.append((residual, normed, projected, mixed, params))
            layer_in = lax.optimization_barrier(output.astype(jnp.bfloat16))
        upstream = out_cotangent[batch_index].astype(jnp.float32)
        for section_index in reversed(range(N_SECTION)):
            residual, normed, projected, mixed, params = saved[section_index]
            upper_lower = upstream.astype(jnp.bfloat16)
            grad_out[section_index] = grad_out[section_index] + lax.dot_general(mixed, upper_lower, contract_rows, preferred_element_type=jnp.float32)
            d_mixed = lax.dot_general(upper_lower, out_weight[section_index], contract_cols, preferred_element_type=jnp.float32)
            d_projected, param_grads = mixer_grads(projected, params, fill_rows, link_rows, d_mixed)
            d_low = d_projected.astype(jnp.bfloat16)
            grad_in[section_index] = grad_in[section_index] + lax.dot_general(normed, d_low, contract_rows, preferred_element_type=jnp.float32)
            d_normed = lax.dot_general(d_low, in_weight[section_index], contract_cols, preferred_element_type=jnp.float32)
            unused, pull_norm = jax.vjp(norm_map, residual, norm_gain[section_index])
            d_residual, d_gain = pull_norm(d_normed)
            grad_gain[section_index] = grad_gain[section_index] + d_gain
            if grad_small[section_index] is None:
                grad_small[section_index] = param_grads
            else:
                grad_small[section_index] = jax.tree.map(jnp.add, grad_small[section_index], param_grads)
            input_grad = upstream + d_residual
            input_grads[section_index].append(input_grad)
            upstream = lax.optimization_barrier(input_grad.astype(jnp.bfloat16)).astype(jnp.float32)
    section_outputs = jnp.stack([jnp.stack(outputs_all[section_index]) for section_index in range(N_SECTION)])
    section_input_grads = jnp.stack([jnp.stack(input_grads[section_index]) for section_index in range(N_SECTION)])
    small_stacks = [jnp.stack([grad_small[section_index][member] for section_index in range(N_SECTION)]) for member in range(6)]
    return (section_outputs, section_input_grads, jnp.stack(grad_in), jnp.stack(grad_out), jnp.stack(grad_gain), small_stacks[0], small_stacks[1], small_stacks[2], small_stacks[3], small_stacks[4], small_stacks[5])
```

```python
import functools

import jax
import jax.numpy as jnp
from jax import lax
from jax.experimental import pallas as pl
from jax.experimental.pallas import tpu as pltpu
from jax.sharding import PartitionSpec as P

EPSILON = 1e-05
F32 = jnp.float32
BF16 = jnp.bfloat16
NN = (((1,), (0,)), ((), ()))
NT = (((1,), (1,)), ((), ()))
TN = (((0,), (0,)), ((), ()))
PACK = 4
VMEM_LIMIT = 56 * 1024 * 1024


def shifted_2(x, axis, by):
    peers = lax.axis_size(axis)
    pairs = [(i, i + by) for i in range(peers) if 0 <= i + by < peers]
    return lax.ppermute(x, axis, pairs)


def norm_map(values, gain_row):
    return (
        values * lax.rsqrt(jnp.mean(values * values, axis=-1, keepdims=True) + EPSILON) * gain_row
    )


def mm(left, right, dims):
    return lax.dot_general(left, right, dims, preferred_element_type=F32)


def split(values, parts):
    terms = []
    for _ in range(parts - 1):
        head = values.astype(BF16)
        terms.append(head)
        values = values - head.astype(F32)
    terms.append(values.astype(BF16))
    return terms


def mm3(left, right, dims):
    return (
        mm(left[0], right[0], dims) + mm(left[1], right[0], dims) + mm(left[0], right[1], dims)
    )


def mm_exact(left, right, dims, parts=3):
    if left.dtype == BF16:
        return sum(mm(left, term, dims) for term in split(right, parts))
    return sum(mm(term, right, dims) for term in split(left, parts))


def sigmoid(values):
    return 1.0 / (1.0 + jnp.exp(-values))


class Slot:
    def __init__(self, sizes, fill_ref, link_ref, proj_ref, cw_ref, cb_ref, dtb_ref, alog_ref, expand_ref):
        rows, groups, inner, conv, heads = sizes
        length = rows // groups
        width = rows * PACK
        self.rows, self.width = rows, width
        self.inner, self.conv, self.heads = inner, conv, heads
        self.proj_ref, self.cw_ref, self.cb_ref = proj_ref, cw_ref, cb_ref
        slot = pl.program_id(0)
        row = lax.broadcasted_iota(jnp.int32, (rows, width), 0)
        lane = lax.broadcasted_iota(jnp.int32, (rows, width), 1)
        lane_in = lane % rows
        row_seg = jnp.zeros((rows, width), jnp.int32)
        lane_seg = jnp.zeros((rows, width), jnp.int32)
        linked = jnp.zeros((rows, width), jnp.int32)
        filled = jnp.zeros((rows, width), jnp.int32)
        segment = jnp.int32(0)
        for group in range(groups):
            link = link_ref[slot, group]
            if group:
                segment = segment + (1 - link)
            row_here = (row // length) == group
            row_seg = jnp.where(row_here, segment, row_seg)
            lane_seg = jnp.where((lane_in // length) == group, segment, lane_seg)
            linked = jnp.where(row_here, link, linked)
            filled = jnp.where(row_here, fill_ref[slot, group], filled)
        within = row % length
        self.valid = (within < filled).astype(F32)
        self.keeps = [
            jnp.where(
                (row >= lag) & ((within >= lag) | (linked == 1)), 1.0, 0.0
            ).astype(F32)
            for lag in range(1, cw_ref.shape[0])
        ]
        same = row_seg == lane_seg
        self.causal = same & (lane_in <= row)
        self.anti = same & (lane_in >= row)
        self.eye = lane_in == row
        self.block = [(lane // rows == part).astype(F32).astype(BF16) for part in range(PACK)]
        low = lax.broadcasted_iota(jnp.int32, (rows, rows), 0)
        high = lax.broadcasted_iota(jnp.int32, (rows, rows), 1)
        self.tril = (low >= high).astype(F32).astype(BF16)
        self.triu = (low <= high).astype(F32).astype(BF16)
        self.bc_at = inner + inner
        self.bc_pre = self.conv_pre(inner, self.bc_at)
        bc = self.bc_pre * sigmoid(self.bc_pre)
        state = (conv - inner) // 2
        self.b_split = split(bc[:, :state], 2)
        self.c_split = split(bc[:, state:], 2)
        self.b_tall = [jnp.concatenate([term] * PACK, axis=0) for term in self.b_split]
        self.scores = mm3(self.c_split, self.b_tall, NT)
        self.dt_in = proj_ref[:, inner + conv :] + dtb_ref[...]
        self.step = jnp.maximum(self.dt_in, 0.0) + jnp.log1p(jnp.exp(-jnp.abs(self.dt_in)))
        self.rate = -jnp.exp(alog_ref[...])
        self.log_decay = self.step * self.rate
        cumulative = mm_exact(self.tril, self.log_decay, NN)
        self.spread = mm_exact(
            jnp.concatenate([cumulative, self.step], axis=0), expand_ref[...], NN
        )

    def conv_pre(self, at, proj_at):
        width = self.width
        conv_in = self.proj_ref[:, pl.ds(proj_at, width)]
        taps = self.cw_ref[:, pl.ds(at, width)]
        pre = self.cb_ref[:, pl.ds(at, width)] + taps[0:1] * conv_in
        for lag, keep in enumerate(self.keeps, 1):
            pre = pre + taps[lag : lag + 1] * (pltpu.roll(conv_in, lag, 0) * keep)
        return pre

    def diagonal(self, terms):
        return [
            jnp.concatenate([term * mask for mask in self.block], axis=0) for term in terms
        ]

    def decay(self, cum):
        across = jnp.sum(jnp.where(self.eye, cum, 0.0), axis=0, keepdims=True)
        return jnp.exp(jnp.where(self.causal, cum - across, -1e30)), across


def forward_kernel(
    sizes, fill_ref, link_ref, proj_ref, cw_ref, cb_ref, dtb_ref, alog_ref, skip_ref, gain_ref,
    expand_ref, mixed_ref, spread_ref, gated_ref,
):
    slot = Slot(sizes, fill_ref, link_ref, proj_ref, cw_ref, cb_ref, dtb_ref, alog_ref, expand_ref)
    rows, width, inner = slot.rows, slot.width, slot.inner
    spread_ref[...] = slot.spread
    steps = inner // width

    def one_pack(index, total):
        at = pl.multiple_of(index * width, width)
        here = pl.ds(at, width)
        pre = slot.conv_pre(at, pl.multiple_of(inner + at, width))
        xs = pre * sigmoid(pre)
        decay, _ = slot.decay(spread_ref[:rows, here])
        weights = split(slot.scores * decay, 2)
        scaled = slot.diagonal(split(xs * spread_ref[rows:, here], 2))
        scanned = mm3(weights, scaled, NN) + skip_ref[:, here] * xs
        gate = proj_ref[:, here]
        gated = scanned * (gate * sigmoid(gate))
        gated_ref[:, here] = gated
        return total + gated * gated

    total = lax.fori_loop(0, steps, one_pack, jnp.zeros((rows, width), F32))
    mean = jnp.sum(total, axis=1, keepdims=True) * (1.0 / inner)
    scale = slot.valid * lax.rsqrt(mean + EPSILON)

    def one_store(index, carry):
        here = pl.ds(pl.multiple_of(index * width, width), width)
        mixed_ref[:, here] = (gated_ref[:, here] * scale * gain_ref[:, here]).astype(BF16)
        return carry

    lax.fori_loop(0, steps, one_store, 0)


def backward_kernel(
    sizes, fill_ref, link_ref, proj_ref, dmix_ref, cw_ref, cb_ref, dtb_ref, alog_ref, skip_ref,
    gain_ref, expand_ref, collect_ref, dproj_ref, dcw_ref, dcb_ref, ddt_ref, dalog_ref, dskip_ref,
    dgain_ref, spread_ref, pre_ref, scan_ref, decay_ref,
):
    @pl.when(pl.program_id(0) == 0)
    def _():
        for ref in (dcw_ref, dcb_ref, ddt_ref, dalog_ref, dskip_ref, dgain_ref):
            ref[...] = jnp.zeros_like(ref)

    slot = Slot(sizes, fill_ref, link_ref, proj_ref, cw_ref, cb_ref, dtb_ref, alog_ref, expand_ref)
    rows, width, inner, conv = slot.rows, slot.width, slot.inner, slot.conv
    spread_ref[...] = slot.spread
    steps = inner // width
    c_tall = [jnp.concatenate([term] * PACK, axis=0) for term in slot.c_split]
    scores_back = mm3(slot.b_split, c_tall, NT)

    def first(index, totals):
        square, product = totals
        at = pl.multiple_of(index * width, width)
        here = pl.ds(at, width)
        pre = slot.conv_pre(at, pl.multiple_of(inner + at, width))
        pre_ref[:, here] = pre
        xs = pre * sigmoid(pre)
        decay, _ = slot.decay(spread_ref[:rows, here])
        decay_ref[:, here] = decay
        weights = split(slot.scores * decay, 2)
        scaled = slot.diagonal(split(xs * spread_ref[rows:, here], 2))
        scanned = mm3(weights, scaled, NN) + skip_ref[:, here] * xs
        scan_ref[:, here] = scanned
        gate = proj_ref[:, here]
        gated = scanned * (gate * sigmoid(gate))
        scaled_grad = dmix_ref[:, here] * slot.valid * gain_ref[:, here]
        return square + gated * gated, product + scaled_grad * gated

    zeros = jnp.zeros((rows, width), F32)
    square, product = lax.fori_loop(0, steps, first, (zeros, zeros))
    scale = lax.rsqrt(jnp.sum(square, axis=1, keepdims=True) * (1.0 / inner) + EPSILON)
    pull = scale * scale * scale * (jnp.sum(product, axis=1, keepdims=True) * (1.0 / inner))

    def conv_back(at, proj_at, pre, grad):
        gate = sigmoid(pre)
        grad = grad * (gate * (1.0 + pre * (1.0 - gate)))
        here = pl.ds(at, width)
        conv_in = proj_ref[:, pl.ds(proj_at, width)]
        taps = cw_ref[:, here]
        dcb_ref[:, here] += jnp.sum(grad, axis=0, keepdims=True)
        dcw_ref[0:1, here] += jnp.sum(grad * conv_in, axis=0, keepdims=True)
        back = taps[0:1] * grad
        for lag, keep in enumerate(slot.keeps, 1):
            kept = grad * keep
            dcw_ref[lag : lag + 1, here] += jnp.sum(
                kept * pltpu.roll(conv_in, lag, 0), axis=0, keepdims=True
            )
            back = back + pltpu.roll(taps[lag : lag + 1] * kept, rows - lag, 0)
        dproj_ref[:, pl.ds(proj_at, width)] = back.astype(BF16)

    def second(index, carry):
        d_scores, sums = carry
        at = pl.multiple_of(index * width, width)
        here = pl.ds(at, width)
        gate = proj_ref[:, here]
        opened = sigmoid(gate)
        scanned = scan_ref[:, here]
        gated = scanned * (gate * opened)
        d_norm = dmix_ref[:, here] * slot.valid
        d_gated = scale * (d_norm * gain_ref[:, here]) - gated * pull
        dgain_ref[:, here] += jnp.sum(d_norm * gated * scale, axis=0, keepdims=True)
        d_scan = d_gated * (gate * opened)
        dproj_ref[:, here] = (
            d_gated * scanned * (opened * (1.0 + gate * (1.0 - opened)))
        ).astype(BF16)
        pre = pre_ref[:, here]
        xs = pre * sigmoid(pre)
        dskip_ref[:, here] += jnp.sum(d_scan * xs, axis=0, keepdims=True)
        cum = spread_ref[:rows, here]
        step = spread_ref[rows:, here]
        decay = decay_ref[:, here]
        scaled = slot.diagonal(split(xs * step, 2))
        d_split = split(d_scan, 2)
        d_weights = mm3(d_split, scaled, NT)
        by_decay = d_weights * decay
        d_scores = d_scores + by_decay
        across = jnp.sum(jnp.where(slot.eye, cum, 0.0), axis=0, keepdims=True)
        decay_back = jnp.exp(jnp.where(slot.anti, across - cum, -1e30))
        weights_back = split(scores_back * decay_back, 2)
        d_scaled = mm3(weights_back, slot.diagonal(d_split), NN)
        flow = by_decay * slot.scores
        net = flow - jnp.where(slot.eye, jnp.sum(flow, axis=0, keepdims=True), 0.0)
        both = jnp.concatenate([net, d_scaled * xs], axis=0)
        sums = sums + mm_exact(both, collect_ref[pl.ds(at, width), :], NN, 2)
        grad = d_scaled * step + skip_ref[:, here] * d_scan
        conv_back(at, pl.multiple_of(inner + at, width), pre, grad)
        return d_scores, sums

    d_scores, sums = lax.fori_loop(
        0, steps, second, (zeros, jnp.zeros((2 * rows, slot.heads), F32))
    )
    d_split = split(d_scores, 2)
    d_c = mm3(d_split, slot.b_tall, NN)
    d_b_tall = mm3(d_split, slot.c_split, TN)
    d_b = d_b_tall[:rows]
    for part in range(1, PACK):
        d_b = d_b + d_b_tall[part * rows : (part + 1) * rows]
    conv_back(inner, slot.bc_at, slot.bc_pre, jnp.concatenate([d_b, d_c], axis=1))
    d_decay = mm_exact(slot.triu, sums[:rows], NN)
    d_step = sums[rows:] + d_decay * slot.rate
    dalog_ref[...] += jnp.sum(d_decay * slot.log_decay, axis=0, keepdims=True)
    d_dt = d_step * sigmoid(slot.dt_in)
    ddt_ref[...] += jnp.sum(d_dt, axis=0, keepdims=True)
    dproj_ref[:, inner + conv :] = d_dt.astype(BF16)


def whole(array):
    return pl.BlockSpec(array.shape, lambda slot: (0,) * array.ndim)


def per_slot(rows, columns):
    return pl.BlockSpec((rows, columns), lambda slot: (slot, 0))


def mixer_sizes(projected, fill, params):
    taps, bias, dt_bias, _, _, gain = params
    return (
        projected.shape[0] // fill.shape[0],
        fill.shape[1],
        gain.shape[1],
        bias.shape[1],
        dt_bias.shape[1],
    )


def mixer_forward(projected, fill, link, params, expand):
    sizes = mixer_sizes(projected, fill, params)
    rows, _, inner, _, _ = sizes
    smem = pl.BlockSpec(memory_space=pltpu.SMEM)
    return pl.pallas_call(
        functools.partial(forward_kernel, sizes),
        grid=(fill.shape[0],),
        in_specs=[smem, smem, per_slot(rows, projected.shape[1])]
        + [whole(item) for item in params]
        + [whole(expand)],
        out_specs=per_slot(rows, inner),
        out_shape=jax.ShapeDtypeStruct((projected.shape[0], inner), BF16),
        scratch_shapes=[pltpu.VMEM((2 * rows, inner), F32), pltpu.VMEM((rows, inner), F32)],
        compiler_params=pltpu.CompilerParams(vmem_limit_bytes=VMEM_LIMIT),
        name="mixer_forward",
    )(fill, link, projected, *params, expand)


def mixer_backward(projected, d_mixed, fill, link, params, expand, collect):
    sizes = mixer_sizes(projected, fill, params)
    rows, _, inner, conv, heads = sizes
    smem = pl.BlockSpec(memory_space=pltpu.SMEM)
    taps = params[0].shape[0]
    smalls = [(taps, conv), (1, conv), (1, heads), (1, heads), (1, inner), (1, inner)]
    return pl.pallas_call(
        functools.partial(backward_kernel, sizes),
        grid=(fill.shape[0],),
        in_specs=[smem, smem, per_slot(rows, projected.shape[1]), per_slot(rows, inner)]
        + [whole(item) for item in params]
        + [whole(expand), whole(collect)],
        out_specs=[per_slot(rows, projected.shape[1])]
        + [pl.BlockSpec(shape, lambda slot: (0, 0)) for shape in smalls],
        out_shape=[jax.ShapeDtypeStruct(projected.shape, BF16)]
        + [jax.ShapeDtypeStruct(shape, F32) for shape in smalls],
        scratch_shapes=[pltpu.VMEM((2 * rows, inner), F32)]
        + [pltpu.VMEM((rows, inner), F32)] * 3,
        compiler_params=pltpu.CompilerParams(vmem_limit_bytes=VMEM_LIMIT),
        name="mixer_backward",
    )(fill, link, projected, d_mixed, *params, expand, collect)


def on_device(
    tokens_in,
    out_cotangent,
    in_weight,
    out_weight,
    norm_gain,
    conv_weight,
    conv_bias,
    dt_bias,
    a_log,
    skip_gain,
    gate_gain,
    group_fill,
    group_link,
):
    section_count = lax.axis_size("section")
    section_index = lax.axis_index("section")
    is_first = section_index == 0
    is_last = section_index == section_count - 1
    micro_count, slot_rows, model = tokens_in.shape
    heads, inner = dt_bias.shape[1], gate_gain.shape[1]
    head_size = inner // heads
    expand = jnp.repeat(jnp.eye(heads, dtype=BF16), head_size, axis=1)
    collect = jnp.repeat(jnp.eye(heads, dtype=BF16), head_size, axis=0)
    params = (
        conv_weight[0], conv_bias, dt_bias, a_log, jnp.repeat(skip_gain, head_size, axis=1),
        gate_gain,
    )
    weight_in = lax.all_gather(in_weight[0], "dp", axis=0, tiled=True)
    weight_out = lax.all_gather(out_weight[0], "dp", axis=0, tiled=True)
    own_rows = tokens_in.reshape(-1, model)
    own_grad = out_cotangent.reshape(-1, model)

    layer_in = own_rows
    for step in range(section_count):
        residual = layer_in.astype(F32)
        normed = norm_map(residual, norm_gain).astype(BF16)
        projected = mm(normed, weight_in, NN)
        mixed = mixer_forward(projected, group_fill, group_link, params, expand)
        output = residual + mm(mixed, weight_out, NN)
        if step < section_count - 1:
            received = shifted_2(output.astype(BF16), "section", 1)
            layer_in = jnp.where(is_first, own_rows, received)

    up_low = own_grad
    for step in range(section_count):
        upstream = up_low.astype(F32)
        d_mixed = mm(up_low, weight_out, NT)
        pulled = mixer_backward(
            projected, d_mixed, group_fill, group_link, params, expand, collect
        )
        d_low = pulled[0]
        d_normed = mm(d_low, weight_in, NT)
        _, pull_norm = jax.vjp(norm_map, residual, norm_gain)
        d_residual, d_gain = pull_norm(d_normed)
        input_grad = upstream + d_residual
        if step < section_count - 1:
            received = shifted_2(input_grad.astype(BF16), "section", -1)
            up_low = jnp.where(is_last, own_grad, received)

    shard_out = lax.psum_scatter(
        mm(mixed, up_low, TN).astype(BF16), "dp", scatter_dimension=0, tiled=True
    ).astype(F32)
    shard_in = lax.psum_scatter(
        mm(normed, d_low, TN).astype(BF16), "dp", scatter_dimension=0, tiled=True
    ).astype(F32)
    smalls = (d_gain,) + tuple(pulled[1:])
    flat = jnp.concatenate([item.reshape(-1) for item in smalls])
    flat = lax.psum(flat, "dp")
    summed, at = [], 0
    for item in smalls:
        summed.append(flat[at : at + item.size].reshape(item.shape))
        at += item.size
    gain_sum, taps_sum, bias_sum, dt_sum, alog_sum, skip_sum, gate_sum = summed
    skip_sum = skip_sum.reshape(1, heads, head_size).sum(axis=2)
    shape = (1, micro_count, slot_rows, model)
    return (
        output.reshape(shape),
        input_grad.reshape(shape),
        shard_in[None],
        shard_out[None],
        gain_sum,
        taps_sum[None],
        bias_sum,
        dt_sum,
        alog_sum,
        skip_sum,
        gate_sum,
    )


def solution(mesh):
    in_specs = (
        P(None, "dp", None),
        P(None, "dp", None),
        P("section", "dp", None),
        P("section", "dp", None),
        P("section", None),
        P("section", None, None),
        P("section", None),
        P("section", None),
        P("section", None),
        P("section", None),
        P("section", None),
        P(None, "dp"),
        P(None, "dp"),
    )
    out_specs = (
        P("section", None, "dp", None),
        P("section", None, "dp", None),
        P("section", "dp", None),
        P("section", "dp", None),
        P("section", None),
        P("section", None, None),
        P("section", None),
        P("section", None),
        P("section", None),
        P("section", None),
        P("section", None),
    )
    return jax.shard_map(
        on_device, mesh=mesh, in_specs=in_specs, out_specs=out_specs, check_vma=False
    )
```
